32 devices in a mesh: ctx: 8 (over z, y), tp: 4 (over x, core).
Axes of the slice: x: 2, y: 2, z: 4, core: 2. Of those that a mesh axis runs over, the one named last changes fastest.
Arguments:
- queries: bfloat16 [4096, 8192], P('ctx', 'tp'), may hold values from -6 to 6
- keys: bfloat16 [4096, 1024], P('ctx', 'tp'), may hold values from -6 to 6
- values: bfloat16 [4096, 1024], P('ctx', 'tp'), may hold values from -6 to 6
- block_plan: int32 [8, 4], replicated, may hold values from 0 to 7, as said below
- doc_lengths: int32 [16], replicated, may hold values from 1 to 2048, 4096 in all
- scan_input: bfloat16 [4096, 16384], P('ctx', 'tp'), may hold values from -6 to 6
- gate_input: bfloat16 [4096, 16384], P('ctx', 'tp'), may hold values from -600 to 600
- step_size: bfloat16 [4096, 256], P('ctx', 'tp'), may hold values from 0 to 6
- decay_rate: float32 [256], P('tp'), may hold values from 0.05 to 1.5
- state_in: bfloat16 [4096, 16], P('ctx'), may hold values from -6 to 6
- state_out: bfloat16 [4096, 16], P('ctx'), may hold values from -6 to 6
- skip_gain: float32 [256], P('tp'), may hold values from 0.5 to 1.5
- norm_gain: float32 [16384], P('tp'), may hold values from 0.5 to 1.5
Outputs:
- attn_out: bfloat16 [4096, 8192], P('ctx', 'tp')
- mamba_out: bfloat16 [4096, 16384], P('ctx', 'tp')
The draws below stay inside these ranges and needn't reach their ends.
Inputs may be any that keep to these rules, and one draw needn't show every extreme that they name: `block_plan`: each row lists 4 distinct offsets, the first of them 0.
All inputs are finite; a program needn't handle non-finite values.
Results may differ from the reference program's by a relative error of at most 0.007.
Values may be sent and summed in bfloat16 or wider, within the bound.
A program may use at most 128 MiB of HBM per device.

```python
import math
import jax
import jax.numpy as jnp
import numpy as np
from jax import lax

QUERY_HEADS = 64
KEY_VALUE_HEADS = 8
HEAD_WIDTH = 128
INNER = 16384
STATE_WIDTH = 16
DECAY_CHANNELS = 64
SPAN = 8
PICKED_BLOCKS = 4
BLOCK_TOKENS = 512
TOKEN_TOTAL = 4096
BLOCK_TOTAL = 8
NDOC = 16
DOCMAX = 2048
SCAN_HEAD_COUNT = 256


def log_uniform(key, shape, low, high):
    return jnp.exp(jax.random.uniform(key, shape, jnp.float32, jnp.log(low), jnp.log(high)))


def draw_queries(key, part):
    start_point = jnp.clip(jax.random.normal(jax.random.fold_in(key, 11), (TOKEN_TOTAL, QUERY_HEADS * HEAD_WIDTH), jnp.float32), -6.0, 6.0)
    return start_point.astype(jnp.bfloat16)


def draw_keys(key, part):
    start_point = jnp.clip(jax.random.normal(jax.random.fold_in(key, 12), (TOKEN_TOTAL, KEY_VALUE_HEADS * HEAD_WIDTH), jnp.float32), -6.0, 6.0)
    return start_point.astype(jnp.bfloat16)


def draw_block_plan(key, part):
    scores = jax.random.randint(jax.random.fold_in(key, 13), (BLOCK_TOTAL, SPAN - 1), 0, 1 << 20) * SPAN
    scores = scores + jnp.arange(SPAN - 1, dtype=jnp.int32)[None, :]
    scores = scores.at[0, SPAN - 2].set(-1)
    ranking = jnp.argsort(scores, axis=1)
    picked = (ranking[:, :PICKED_BLOCKS - 1] + 1).astype(jnp.int32)
    return jnp.concatenate([jnp.zeros((BLOCK_TOTAL, 1), jnp.int32), picked], axis=1)


def head_law(key):
    share = 0.5
    slow_heads = jax.random.uniform(jax.random.fold_in(key, 5301), (SCAN_HEAD_COUNT,), jnp.float32) < share
    rate = jnp.where(slow_heads, log_uniform(jax.random.fold_in(key, 5302), (SCAN_HEAD_COUNT,), 0.05, 0.09), log_uniform(jax.random.fold_in(key, 5303), (SCAN_HEAD_COUNT,), 0.5, 1.5))
    step_start_value = jnp.where(slow_heads, log_uniform(jax.random.fold_in(key, 5304), (SCAN_HEAD_COUNT,), 0.002, 0.004), log_uniform(jax.random.fold_in(key, 5305), (SCAN_HEAD_COUNT,), 0.02, 0.05))
    return (rate, step_start_value)


def draw_decay_rate(key, part):
    rate, step_start_value = head_law(key)
    return rate.astype(jnp.float32)


def draw_step_size(key, part):
    rate, step_start_value = head_law(key)
    coarse_scores = log_uniform(jax.random.fold_in(key, 5306), (TOKEN_TOTAL, SCAN_HEAD_COUNT), 0.5, 2.0)
    token_runs = jax.random.randint(jax.random.fold_in(key, 5307), (TOKEN_TOTAL,), 0, 4 * BLOCK_TOKENS) == 0
    value_result = step_start_value[None, :] * coarse_scores + 5.0 * token_runs.astype(jnp.float32)[:, None]
    return value_result.astype(jnp.bfloat16)


def draw_gate_input(key, part):
    channel_scale = 10.0 ** (jnp.arange(INNER, dtype=jnp.float32) / INNER)
    channel_scale = channel_scale * log_uniform(jax.random.fold_in(key, 21), (INNER,), 0.7, 1.4)
    row_scale = log_uniform(jax.random.fold_in(key, 22), (TOKEN_TOTAL, 1), 1.0, 10.0)
    start_point = jnp.clip(jax.random.normal(jax.random.fold_in(key, 24), (TOKEN_TOTAL, INNER), jnp.float32), -4.0, 4.0)
    return (start_point * channel_scale[None, :] * row_scale).astype(jnp.bfloat16)


def level_of(own_key, shape, pieces, smallest, high):
    level, own = 1.0, jax.random.fold_in(own_key, 6)
    for axis_at, blocks in pieces:
        steps = jnp.exp(jax.random.uniform(jax.random.fold_in(own, axis_at), (blocks,), jnp.float32, smallest / len(pieces), high / len(pieces)))
        level = level * jnp.repeat(steps, shape[axis_at] // blocks).reshape([-1 if axis == axis_at else 1 for axis in range(len(shape))])
    return level


def split_up(amount, total, limit, skew):
    loads = [(1 << 20) // math.isqrt(standing ** skew) + 1 for standing in range(2, amount + 1)]
    rest, given = total - limit - (amount - 1), [1] * (amount - 1)
    while rest > 0:
        movable = [i for i in range(amount - 1) if given[i] < limit]
        mass, budget = sum([loads[i] for i in movable]), rest
        for i in movable:
            more = min(limit - given[i], max(1, budget * loads[i] // mass), rest)
            given[i] = given[i] + more
            rest = rest - more
    return np.array([limit] + given)


def uneven(rng, number_of, total, bound, lean):
    if number_of == 2:
        one = jax.random.randint(rng, (), max(1, total - bound), min(bound, total - 1) + 1)
        return jnp.stack([one, total - one])
    sizes = jnp.asarray(split_up(number_of, total, bound, lean), jnp.int32)
    couples = (number_of - 1) // 2
    donor, taker = sizes[1:1 + 2 * couples:2], sizes[2:2 + 2 * couples:2]
    room = jnp.minimum(donor - 1, bound - taker)
    shifted = jax.random.randint(jax.random.fold_in(rng, 1), (couples,), 0, 1 << 20) % (room + 1)
    sizes = sizes.at[1:1 + 2 * couples:2].set(donor - shifted).at[2:2 + 2 * couples:2].set(taker + shifted)
    return sizes[jax.random.permutation(jax.random.fold_in(rng, 2), number_of)]


def scatter_about(rng, shape, deviation, limit, pieces=(), kind=jnp.bfloat16):
    drawn = jax.random.normal(rng, shape, jnp.float32) * deviation
    if len(pieces) > 0:
        drawn = level_of(rng, shape, pieces, -0.22, 0.18) * drawn
    return jnp.clip(drawn, min=-limit, max=limit).astype(kind)


def setup_inputs(seed: int = 0) -> dict:
    splits = jax.random.split(jax.random.key(seed), 14)
    queries = draw_queries(jax.random.fold_in(splits[13], 71), 0)
    keys = draw_keys(jax.random.fold_in(splits[13], 71), 0)
    values = scatter_about(splits[2], (TOKEN_TOTAL, KEY_VALUE_HEADS * HEAD_WIDTH), 1.0, 6.0, ((0, 8), (1, 4)))
    block_plan = draw_block_plan(jax.random.fold_in(splits[13], 71), 0)
    doc_lengths = uneven(splits[4], NDOC, TOKEN_TOTAL, DOCMAX, 2).astype(jnp.int32)
    scan_input = scatter_about(splits[5], (TOKEN_TOTAL, INNER), 1.0, 6.0, ((0, 8), (1, 4)))
    gate_input = draw_gate_input(jax.random.fold_in(splits[13], 71), 0)
    step_size = draw_step_size(jax.random.fold_in(splits[13], 71), 0)
    decay_rate = draw_decay_rate(jax.random.fold_in(splits[13], 71), 0)
    state_in = scatter_about(splits[9], (TOKEN_TOTAL, STATE_WIDTH), 1.0, 6.0, ((0, 8),))
    state_out = scatter_about(splits[10], (TOKEN_TOTAL, STATE_WIDTH), 1.0, 6.0, ((0, 8),))
    skip_gain = jnp.clip(0.5 + 1.0 * jax.random.uniform(splits[11], (SCAN_HEAD_COUNT,), jnp.float32) ** level_of(splits[11], (SCAN_HEAD_COUNT,), ((0, 4),), -0.2, 0.2), 0.5, 1.5)
    norm_gain = jnp.clip(1.0 + 0.1 * jax.random.normal(splits[12], (INNER,), jnp.float32), 0.5, 1.5)
    return dict(queries=queries, keys=keys, values=values, block_plan=block_plan, doc_lengths=doc_lengths, scan_input=scan_input, gate_input=gate_input, step_size=step_size, decay_rate=decay_rate, state_in=state_in, state_out=state_out, skip_gain=skip_gain, norm_gain=norm_gain)


def doc_index(positions, doc_lengths):
    doc_ends = jnp.cumsum(doc_lengths).astype(jnp.int32)
    return lax.optimization_barrier(jnp.sum((positions[:, None] >= doc_ends[None, :]).astype(jnp.int32), axis=1)).astype(jnp.int32)

def attention(queries, keys, values, block_plan, doc_lengths):
    query_group_width = QUERY_HEADS // KEY_VALUE_HEADS
    scale_factor = HEAD_WIDTH ** (-0.5)
    every_query = queries.reshape(BLOCK_TOTAL, BLOCK_TOKENS, KEY_VALUE_HEADS, query_group_width, HEAD_WIDTH)
    every_key = keys.reshape(BLOCK_TOTAL, BLOCK_TOKENS, KEY_VALUE_HEADS, HEAD_WIDTH)
    every_value = values.reshape(BLOCK_TOTAL, BLOCK_TOKENS, KEY_VALUE_HEADS, HEAD_WIDTH)
    offsets_row = jnp.arange(BLOCK_TOKENS, dtype=jnp.int32)

    def one_block(block_index):
        query_block = lax.dynamic_index_in_dim(every_query, block_index, 0, keepdims=False)
        chosen = block_index - block_plan[block_index]
        valid = chosen >= 0
        clamped_block = jnp.maximum(chosen, 0).astype(jnp.int32)
        picked_keys = every_key[clamped_block].reshape(PICKED_BLOCKS * BLOCK_TOKENS, KEY_VALUE_HEADS, HEAD_WIDTH)
        picked_values = every_value[clamped_block].reshape(PICKED_BLOCKS * BLOCK_TOKENS, KEY_VALUE_HEADS, HEAD_WIDTH)
        query_position = block_index * BLOCK_TOKENS + offsets_row
        key_position = (clamped_block[:, None] * BLOCK_TOKENS + offsets_row[None, :]).reshape(-1)
        key_valid = jnp.repeat(valid, BLOCK_TOKENS)
        allowed = key_valid[None, :] & (key_position[None, :] <= query_position[:, None])
        allowed = allowed & (doc_index(key_position, doc_lengths)[None, :] == doc_index(query_position, doc_lengths)[:, None])
        scores = jnp.einsum('tkgd,skd->kgts', query_block.astype(jnp.float32), picked_keys.astype(jnp.float32)) * scale_factor
        masked = jnp.where(allowed[None, None], scores, -1e+30)
        row_peak = lax.optimization_barrier(jnp.max(masked, axis=-1, keepdims=True))
        weights = jnp.where(allowed[None, None], jnp.exp(masked - row_peak), 0.0)
        denominator = lax.optimization_barrier(jnp.sum(weights, axis=-1))
        rounded = lax.optimization_barrier(weights.astype(jnp.bfloat16)).astype(jnp.float32)
        weighted = jnp.einsum('kgts,skd->tkgd', rounded, picked_values.astype(jnp.float32))
        result = weighted / jnp.transpose(denominator, (2, 0, 1))[..., None]
        return result.astype(jnp.bfloat16).reshape(BLOCK_TOKENS, QUERY_HEADS * HEAD_WIDTH)
    blocks_out = lax.map(one_block, jnp.arange(BLOCK_TOTAL, dtype=jnp.int32))
    return blocks_out.reshape(TOKEN_TOTAL, QUERY_HEADS * HEAD_WIDTH)

def selective_scan(scan_input, gate_input, step_size, decay_rate, state_in, state_out, skip_gain, norm_gain, doc_lengths):
    positions = jnp.arange(TOKEN_TOTAL, dtype=jnp.int32)
    token_doc = doc_index(positions, doc_lengths)
    first_flag = jnp.concatenate([jnp.ones((1,), dtype=bool), token_doc[1:] != token_doc[:-1]])

    def one_token(hidden_state, inputs):
        input_token, gate_token, step_token, in_token, out_token, first_token = inputs
        input_single = input_token.astype(jnp.float32).reshape(SCAN_HEAD_COUNT, DECAY_CHANNELS)
        step_float = step_token.astype(jnp.float32)
        decay = jnp.where(first_token, jnp.float32(0.0), jnp.exp(-decay_rate * step_float))
        drive_value = lax.optimization_barrier((step_float[:, None] * input_single).astype(jnp.bfloat16)).astype(jnp.float32)
        drive = drive_value[:, :, None] * in_token.astype(jnp.float32)[None, None, :]
        hidden_state = decay[:, None, None] * hidden_state + drive
        scan_y = lax.optimization_barrier(jnp.sum(hidden_state * out_token.astype(jnp.float32)[None, None, :], axis=-1)) + skip_gain[:, None] * input_single
        gated = scan_y.reshape(INNER) * jax.nn.silu(gate_token.astype(jnp.float32))
        result = gated * lax.rsqrt(jnp.mean(gated * gated) + 1e-05) * norm_gain
        return (hidden_state, result.astype(jnp.bfloat16))
    starting_state = jnp.zeros((SCAN_HEAD_COUNT, DECAY_CHANNELS, STATE_WIDTH), jnp.float32)
    _, mamba_out = lax.scan(one_token, starting_state, (scan_input, gate_input, step_size, state_in, state_out, first_flag))
    return mamba_out

def reference(queries, keys, values, block_plan, doc_lengths, scan_input, gate_input, step_size, decay_rate, state_in, state_out, skip_gain, norm_gain):
    attn_out = attention(queries, keys, values, block_plan, doc_lengths)
    mamba_out = selective_scan(scan_input, gate_input, step_size, decay_rate, state_in, state_out, skip_gain, norm_gain, doc_lengths)
    return (attn_out, mamba_out)
```

```python
import functools
import math

import jax
import jax.numpy as jnp
from jax import lax
from jax.experimental import pallas as pl
from jax.experimental.pallas import tpu as pltpu
from jax.sharding import PartitionSpec as P

HEAD_WIDTH = 128
SPAN = 8
GROUP = 8
LANES = 128
NEG = -1e30


def from_behind(x, axis, by):
    size = lax.axis_size(axis)
    return lax.ppermute(x, axis, [(i, i + by) for i in range(size - by)])


def pair_lanes(low, high, lane):
    return jnp.where(lane, low, high)


def split_state(state):
    high = state.astype(jnp.bfloat16)
    low = (state - high.astype(jnp.float32)).astype(jnp.bfloat16)
    return jnp.concatenate([high, low], axis=0)


def attention_kernel(width, pieces, active, start, q, *refs):
    keys, values = refs[: 2 * pieces : 2], refs[1 : 2 * pieces : 2]
    out, bias, acc, peak, total = refs[2 * pieces :]
    rows = q.shape[0]
    heads = q.shape[1] // width
    scale = width**-0.5 * math.log2(math.e)
    key_at = lax.broadcasted_iota(jnp.int32, (rows, rows), 0)
    query_at = lax.broadcasted_iota(jnp.int32, (rows, rows), 1)

    def fold(piece):
        seen = key_at - piece * rows >= start[...]
        if piece == 0:
            seen = seen & (key_at <= query_at)
        bias[...] = jnp.where(seen, 0.0, NEG)
        value_t = values[piece][...].T

        def one_head(h, _):
            at = pl.ds(pl.multiple_of(h * width, width), width)
            scores = lax.dot_general(
                keys[piece][...],
                q[:, at],
                (((1,), (1,)), ((), ())),
                preferred_element_type=jnp.float32,
            )
            scores = scores * scale + bias[...]
            top = jnp.max(scores, axis=0, keepdims=True)
            if piece > 0:
                top = jnp.maximum(top, peak[h])
            weights = jnp.exp2(scores - top)
            part = jnp.sum(weights, axis=0, keepdims=True)
            weighted = jnp.dot(
                value_t, weights.astype(jnp.bfloat16), preferred_element_type=jnp.float32
            )
            if piece > 0:
                factor = jnp.exp2(peak[h] - top)
                part = part + total[h] * factor
                weighted = weighted + acc[h] * factor
            peak[h] = top
            total[h] = part
            acc[h] = weighted
            return 0

        lax.fori_loop(0, heads, one_head, 0)

    fold(0)
    for piece in range(1, pieces):
        pl.when(active[piece] > 0)(functools.partial(fold, piece))

    def finish(h, _):
        at = pl.ds(pl.multiple_of(h * width, width), width)
        out[:, at] = (acc[h] / total[h]).T.astype(out.dtype)
        return 0

    lax.fori_loop(0, heads, finish, 0)


def attention(q, blocks, start, active, kv_heads):
    rows = q.shape[0]
    wide = q.shape[1] // kv_heads
    pieces = len(blocks)
    heads = wide // HEAD_WIDTH
    specs = [
        pl.BlockSpec((1, rows), lambda i, a: (0, 0)),
        pl.BlockSpec((rows, wide), lambda i, a: (0, i)),
    ]
    operands = [start, q]
    for key_rows, value_rows, first in blocks:
        specs.append(pl.BlockSpec((rows, HEAD_WIDTH), lambda i, a: (0, i)))
        specs.append(pl.BlockSpec((rows, HEAD_WIDTH), lambda i, a, first=first: (0, first + i)))
        operands += [key_rows, value_rows]
    return pl.pallas_call(
        functools.partial(attention_kernel, HEAD_WIDTH, pieces),
        out_shape=jax.ShapeDtypeStruct(q.shape, jnp.bfloat16),
        grid_spec=pltpu.PrefetchScalarGridSpec(
            num_scalar_prefetch=1,
            grid=(kv_heads,),
            in_specs=specs,
            out_specs=pl.BlockSpec((rows, wide), lambda i, a: (0, i)),
            scratch_shapes=[
                pltpu.VMEM((rows, rows), jnp.float32),
                pltpu.VMEM((heads, HEAD_WIDTH, rows), jnp.float32),
                pltpu.VMEM((heads, 1, rows), jnp.float32),
                pltpu.VMEM((heads, 1, rows), jnp.float32),
            ],
        ),
        cost_estimate=pl.CostEstimate(
            flops=8 * rows * rows * q.shape[1] * 2,
            bytes_accessed=4 * q.size,
            transcendentals=4 * rows * rows * kv_heads * heads,
        ),
        name="attend",
    )(active, *operands)


def scan_kernel(chunk, x, factors, rates_t, state_in, state_in_t, out_twice, start, skip, y, state, mix):
    rows = x.shape[0]
    chunks = rows // chunk
    states = state_in.shape[1]

    @pl.when(pl.program_id(0) == 0)
    def _():
        later = lax.broadcasted_iota(jnp.int32, (chunk, chunk), 0)
        earlier = lax.broadcasted_iota(jnp.int32, (chunk, chunk), 1)
        for c in range(chunks):
            at = pl.ds(c * chunk, chunk)
            both = lax.dot_general(
                out_twice[at, :states],
                state_in[at, :],
                (((1,), (1,)), ((), ())),
                preferred_element_type=jnp.float32,
            )
            seen = (later >= earlier) & (earlier + c * chunk >= start[at, :])
            mix[c] = jnp.where(seen, both, 0.0)

    lane = lax.broadcasted_iota(jnp.int32, (chunk, LANES), 1) < LANES // 2
    lane_row = lax.broadcasted_iota(jnp.int32, (1, LANES), 1) < LANES // 2
    for pair in range(GROUP // 2):
        cols = pl.ds(pair * LANES, LANES)
        a, b = 2 * pair, 2 * pair + 1
        held = None
        for c in range(chunks):
            at = pl.ds(c * chunk, chunk)

            def column(kind, h):
                return factors[0, at, pl.ds(kind * GROUP + h, 1)]

            def wide(kind):
                return pair_lanes(column(kind, a), column(kind, b), lane)

            values = x[at, cols].astype(jnp.float32)
            drive = (wide(3) * values).astype(jnp.bfloat16)

            def local(h):
                gap = jnp.minimum(column(0, h) - rates_t[pl.ds(h, 1), at], 0.0)
                mixing = (jnp.exp(gap) * mix[c]).astype(jnp.bfloat16)
                return jnp.dot(mixing, drive, preferred_element_type=jnp.float32)

            result = pair_lanes(local(a), local(b), lane) + skip[:, cols] * values
            tail = (wide(2) * drive.astype(jnp.float32)).astype(jnp.bfloat16)
            added = jnp.dot(state_in_t[:, at], tail, preferred_element_type=jnp.float32)
            if held is not None:
                result = result + wide(1) * jnp.dot(
                    out_twice[at, :], split_state(held), preferred_element_type=jnp.float32
                )
                last = pl.ds(c * chunk + chunk - 1, 1)
                kept = pair_lanes(
                    factors[0, last, pl.ds(GROUP + a, 1)],
                    factors[0, last, pl.ds(GROUP + b, 1)],
                    lane_row,
                )
                added = added + kept * held
            held = added
            y[at, cols] = result
        state[:, cols] = held


def local_scan(x, factors, rates_t, state_in, state_in_t, out_twice, start, skip, chunk):
    rows, channels = x.shape
    groups = factors.shape[0]
    wide = channels // groups
    states = state_in.shape[1]
    whole = lambda shape: pl.BlockSpec(shape, lambda i: (0, 0))
    return pl.pallas_call(
        functools.partial(scan_kernel, chunk),
        out_shape=(
            jax.ShapeDtypeStruct((rows, channels), jnp.float32),
            jax.ShapeDtypeStruct((states, channels), jnp.float32),
        ),
        grid=(groups,),
        in_specs=[
            pl.BlockSpec((rows, wide), lambda i: (0, i)),
            pl.BlockSpec((1,) + factors.shape[1:], lambda i: (i, 0, 0)),
            pl.BlockSpec((GROUP, rows), lambda i: (i, 0)),
            whole(state_in.shape),
            whole(state_in_t.shape),
            whole(out_twice.shape),
            whole(start.shape),
            pl.BlockSpec((1, wide), lambda i: (0, i)),
        ],
        out_specs=(
            pl.BlockSpec((rows, wide), lambda i: (0, i)),
            pl.BlockSpec((states, wide), lambda i: (0, i)),
        ),
        scratch_shapes=[pltpu.VMEM((rows // chunk, chunk, chunk), jnp.float32)],
        cost_estimate=pl.CostEstimate(
            flops=16 * rows * chunk * channels,
            bytes_accessed=8 * x.size,
            transcendentals=rows * chunk * groups * GROUP,
        ),
        name="local_scan",
    )(x, factors, rates_t, state_in, state_in_t, out_twice, start, skip)


def gate_kernel(y, gate, incoming, reach, out_twice, gated, squares):
    rows = y.shape[0]
    lane = lax.broadcasted_iota(jnp.int32, (rows, LANES), 1) < LANES // 2
    folded = jnp.zeros((rows, LANES), jnp.float32)
    for pair in range(GROUP // 2):
        cols = pl.ds(pair * LANES, LANES)
        wide = pair_lanes(
            reach[0, :, pl.ds(2 * pair, 1)], reach[0, :, pl.ds(2 * pair + 1, 1)], lane
        )
        carried = jnp.dot(
            out_twice[...], split_state(incoming[:, cols]), preferred_element_type=jnp.float32
        )
        g = gate[:, cols].astype(jnp.float32)
        value = (y[:, cols] + wide * carried) * (g / (1.0 + jnp.exp(-g)))
        gated[:, cols] = value
        folded = folded + value * value

    @pl.when(pl.program_id(0) == 0)
    def _():
        squares[...] = folded

    @pl.when(pl.program_id(0) > 0)
    def _():
        squares[...] += folded


def gate_all(y, gate, incoming, reach, out_twice):
    rows, channels = y.shape
    groups = reach.shape[0]
    wide = channels // groups
    return pl.pallas_call(
        gate_kernel,
        out_shape=(
            jax.ShapeDtypeStruct((rows, channels), jnp.float32),
            jax.ShapeDtypeStruct((rows, LANES), jnp.float32),
        ),
        grid=(groups,),
        in_specs=[
            pl.BlockSpec((rows, wide), lambda i: (0, i)),
            pl.BlockSpec((rows, wide), lambda i: (0, i)),
            pl.BlockSpec((incoming.shape[0], wide), lambda i: (0, i)),
            pl.BlockSpec((1,) + reach.shape[1:], lambda i: (i, 0, 0)),
            pl.BlockSpec(out_twice.shape, lambda i: (0, 0)),
        ],
        out_specs=(
            pl.BlockSpec((rows, wide), lambda i: (0, i)),
            pl.BlockSpec((rows, LANES), lambda i: (0, 0)),
        ),
        cost_estimate=pl.CostEstimate(
            flops=80 * y.size, bytes_accessed=10 * y.size, transcendentals=y.size
        ),
        name="gate_all",
    )(y, gate, incoming, reach, out_twice)


def shards(
    queries,
    keys,
    values,
    block_plan,
    doc_lengths,
    scan_input,
    gate_input,
    step_size,
    decay_rate,
    state_in,
    state_out,
    skip_gain,
    norm_gain,
):
    ctx, tp = lax.axis_size("ctx"), lax.axis_size("tp")
    me = lax.axis_index("ctx")
    rows = queries.shape[0]
    heads = decay_rate.shape[0]
    channels = scan_input.shape[1]
    head_dim = channels // heads
    groups = heads // GROUP
    kv_heads = keys.shape[1] // HEAD_WIDTH
    chunk = math.gcd(rows, 256)
    chunks = rows // chunk
    doc_reach = min(ctx - 1, 4 if ctx <= SPAN else SPAN)
    key_reach = min(doc_reach, SPAN - 1)

    window = jnp.concatenate([keys, values], axis=1)
    arrived = [from_behind(window, "ctx", by) for by in range(1, key_reach + 1)]

    offsets = jnp.arange(rows, dtype=jnp.int32)
    positions = me * rows + offsets
    doc_ends = jnp.cumsum(doc_lengths)
    start = jnp.sum(
        jnp.where(doc_ends[None, :] <= positions[:, None], doc_lengths[None, :], 0), axis=1
    ).astype(jnp.int32) - me * rows

    step = step_size.astype(jnp.float32)
    rate = (-decay_rate[None, :] * step).reshape(chunks, chunk, heads)
    lower = jnp.tril(jnp.ones((chunk, chunk), jnp.float32))
    cumulative = jnp.einsum("ts,csh->cth", lower, rate, precision=lax.Precision.HIGHEST)
    start_chunks = start.reshape(chunks, chunk)
    first = jnp.arange(chunks, dtype=jnp.int32)[:, None] * chunk
    enters = jnp.where((start_chunks < first)[..., None], jnp.exp(cumulative), 0.0)
    in_tail = offsets.reshape(chunks, chunk) >= start_chunks[:, -1:]
    tails = jnp.where(in_tail[..., None], jnp.exp(cumulative[:, -1:] - cumulative), 0.0)
    through = jnp.ones((heads,), jnp.float32)
    reach = []
    for c in range(chunks):
        reach.append(enters[c] * through[None, :])
        through = through * enters[c, -1]
    reach = jnp.stack(reach).reshape(rows, groups, GROUP).transpose(1, 0, 2)
    flat = cumulative.reshape(rows, heads)
    factors = (
        jnp.stack([flat, enters.reshape(rows, heads), tails.reshape(rows, heads), step], axis=1)
        .reshape(rows, 4, groups, GROUP)
        .transpose(2, 0, 1, 3)
        .reshape(groups, rows, 4 * GROUP)
    )
    out_twice = jnp.concatenate([state_out, state_out], axis=1)
    skip = jnp.repeat(skip_gain, head_dim)[None, :]
    y, end_state = local_scan(
        scan_input,
        factors,
        flat.T,
        state_in,
        state_in.T,
        out_twice,
        start[:, None],
        skip,
        chunk,
    )

    states = [from_behind(end_state, "ctx", by) for by in range(1, doc_reach + 1)]
    passes = [from_behind(through, "ctx", by) for by in range(1, doc_reach)]
    incoming = states[-1]
    for state, passed in zip(states[-2::-1], passes[::-1]):
        incoming = state + jnp.repeat(passed, head_dim)[None, :] * incoming

    plan_row = lax.dynamic_index_in_dim(block_plan, me, 0, keepdims=False)
    back = jnp.arange(key_reach + 1, dtype=jnp.int32)
    active = (
        jnp.any(plan_row[None, :] == back[:, None], axis=1)
        & (me >= back)
        & (start[0] < -(back - 1) * rows)
    ).astype(jnp.int32)
    blocks = [(keys, values, 0)] + [(kv, kv, kv_heads) for kv in arrived]
    attn_out = attention(queries, blocks, start[None, :], active, kv_heads)

    gated, squares = gate_all(y, gate_input, incoming, reach, out_twice)
    own = jnp.sum(squares, axis=1).reshape(-1, LANES)
    total = own
    for by in range(1, tp):
        total = total + lax.ppermute(own, "tp", [(i, (i + by) % tp) for i in range(tp)])
    mean = total.reshape(rows) / (channels * tp)
    mamba_out = (gated * lax.rsqrt(mean + 1e-05)[:, None] * norm_gain[None, :]).astype(jnp.bfloat16)
    return (attn_out, mamba_out)


def solution(mesh):
    in_specs = (
        P("ctx", "tp"),
        P("ctx", "tp"),
        P("ctx", "tp"),
        P(),
        P(),
        P("ctx", "tp"),
        P("ctx", "tp"),
        P("ctx", "tp"),
        P("tp"),
        P("ctx", None),
        P("ctx", None),
        P("tp"),
        P("tp"),
    )
    out_specs = (P("ctx", "tp"), P("ctx", "tp"))
    return jax.shard_map(shards, mesh=mesh, in_specs=in_specs, out_specs=out_specs, check_vma=False)
```

```python
import functools
import math

import jax
import jax.numpy as jnp
from jax import lax
from jax.experimental import pallas as pl
from jax.experimental.pallas import tpu as pltpu
from jax.sharding import PartitionSpec as P


HEAD_WIDTH = 128
SPAN = 8
GROUP = 8
LANES = 128
NEG = -1e30


def from_behind(x, axis, by):
    size = lax.axis_size(axis)
    return lax.ppermute(x, axis, [(i, i + by) for i in range(size - by)])


def longest_reach(ctx):
    return min(ctx - 1, 4 if ctx <= SPAN else SPAN)


def pair_lanes(low, high, lane):
    return jnp.where(lane, low, high)


def split_state(state):
    high = state.astype(jnp.bfloat16)
    low = (state - high.astype(jnp.float32)).astype(jnp.bfloat16)
    return jnp.concatenate([high, low], axis=0)


def attention_kernel(width, pieces, active, start, q, *refs):
    keys, values = refs[: 2 * pieces : 2], refs[1 : 2 * pieces : 2]
    out, bias, acc, peak, total = refs[2 * pieces :]
    rows = q.shape[0]
    heads = q.shape[1] // width
    scale = width**-0.5 * math.log2(math.e)
    key_at = lax.broadcasted_iota(jnp.int32, (rows, rows), 0)
    query_at = lax.broadcasted_iota(jnp.int32, (rows, rows), 1)

    def fold(piece):
        seen = key_at - piece * rows >= start[...]
        if piece == 0:
            seen = seen & (key_at <= query_at)
        bias[...] = jnp.where(seen, 0.0, NEG)
        value_t = values[piece][...].T

        def one_head(h, _):
            at = pl.ds(pl.multiple_of(h * width, width), width)
            scores = lax.dot_general(
                keys[piece][...],
                q[:, at],
                (((1,), (1,)), ((), ())),
                preferred_element_type=jnp.float32,
            )
            scores = scores * scale + bias[...]
            top = jnp.max(scores, axis=0, keepdims=True)
            if piece > 0:
                top = jnp.maximum(top, peak[h])
            weights = jnp.exp2(scores - top)
            part = jnp.sum(weights, axis=0, keepdims=True)
            weighted = jnp.dot(
                value_t, weights.astype(jnp.bfloat16), preferred_element_type=jnp.float32
            )
            if piece > 0:
                factor = jnp.exp2(peak[h] - top)
                part = part + total[h] * factor
                weighted = weighted + acc[h] * factor
            peak[h] = top
            total[h] = part
            acc[h] = weighted
            return 0

        lax.fori_loop(0, heads, one_head, 0)

    fold(0)
    for piece in range(1, pieces):
        pl.when(active[piece] > 0)(functools.partial(fold, piece))

    def finish(h, _):
        at = pl.ds(pl.multiple_of(h * width, width), width)
        out[:, at] = (acc[h] / total[h]).T.astype(out.dtype)
        return 0

    lax.fori_loop(0, heads, finish, 0)


def attention(q, blocks, start, active, kv_heads):
    rows = q.shape[0]
    wide = q.shape[1] // kv_heads
    pieces = len(blocks)
    heads = wide // HEAD_WIDTH
    specs = [
        pl.BlockSpec((1, rows), lambda i, a: (0, 0)),
        pl.BlockSpec((rows, wide), lambda i, a: (0, i)),
    ]
    operands = [start, q]
    for key_rows, value_rows, first in blocks:
        specs.append(pl.BlockSpec((rows, HEAD_WIDTH), lambda i, a: (0, i)))
        specs.append(pl.BlockSpec((rows, HEAD_WIDTH), lambda i, a, first=first: (0, first + i)))
        operands += [key_rows, value_rows]
    return pl.pallas_call(
        functools.partial(attention_kernel, HEAD_WIDTH, pieces),
        out_shape=jax.ShapeDtypeStruct(q.shape, jnp.bfloat16),
        grid_spec=pltpu.PrefetchScalarGridSpec(
            num_scalar_prefetch=1,
            grid=(kv_heads,),
            in_specs=specs,
            out_specs=pl.BlockSpec((rows, wide), lambda i, a: (0, i)),
            scratch_shapes=[
                pltpu.VMEM((rows, rows), jnp.float32),
                pltpu.VMEM((heads, HEAD_WIDTH, rows), jnp.float32),
                pltpu.VMEM((heads, 1, rows), jnp.float32),
                pltpu.VMEM((heads, 1, rows), jnp.float32),
            ],
        ),
        cost_estimate=pl.CostEstimate(
            flops=8 * rows * rows * q.shape[1] * 2,
            bytes_accessed=4 * q.size,
            transcendentals=4 * rows * rows * kv_heads * heads,
        ),
        name="attend",
    )(active, *operands)


def scan_kernel(chunk, x, factors, rates_t, state_in, state_in_t, out_twice, start, skip, y, state, mix):
    rows = x.shape[0]
    chunks = rows // chunk
    states = state_in.shape[1]

    @pl.when(pl.program_id(0) == 0)
    def _():
        later = lax.broadcasted_iota(jnp.int32, (chunk, chunk), 0)
        earlier = lax.broadcasted_iota(jnp.int32, (chunk, chunk), 1)
        for c in range(chunks):
            at = pl.ds(c * chunk, chunk)
            both = lax.dot_general(
                out_twice[at, :states],
                state_in[at, :],
                (((1,), (1,)), ((), ())),
                preferred_element_type=jnp.float32,
            )
            seen = (later >= earlier) & (earlier + c * chunk >= start[at, :])
            mix[c] = jnp.where(seen, both, 0.0)

    lane = lax.broadcasted_iota(jnp.int32, (chunk, LANES), 1) < LANES // 2
    lane_row = lax.broadcasted_iota(jnp.int32, (1, LANES), 1) < LANES // 2
    for pair in range(GROUP // 2):
        cols = pl.ds(pair * LANES, LANES)
        a, b = 2 * pair, 2 * pair + 1
        held = None
        for c in range(chunks):
            at = pl.ds(c * chunk, chunk)

            def column(kind, h):
                return factors[0, at, pl.ds(kind * GROUP + h, 1)]

            def wide(kind):
                return pair_lanes(column(kind, a), column(kind, b), lane)

            values = x[at, cols].astype(jnp.float32)
            drive = (wide(3) * values).astype(jnp.bfloat16)

            def local(h):
                gap = jnp.minimum(column(0, h) - rates_t[pl.ds(h, 1), at], 0.0)
                mixing = (jnp.exp(gap) * mix[c]).astype(jnp.bfloat16)
                return jnp.dot(mixing, drive, preferred_element_type=jnp.float32)

            result = pair_lanes(local(a), local(b), lane) + skip[:, cols] * values
            tail = (wide(2) * drive.astype(jnp.float32)).astype(jnp.bfloat16)
            added = jnp.dot(state_in_t[:, at], tail, preferred_element_type=jnp.float32)
            if held is not None:
                result = result + wide(1) * jnp.dot(
                    out_twice[at, :], split_state(held), preferred_element_type=jnp.float32
                )
                last = pl.ds(c * chunk + chunk - 1, 1)
                kept = pair_lanes(
                    factors[0, last, pl.ds(GROUP + a, 1)],
                    factors[0, last, pl.ds(GROUP + b, 1)],
                    lane_row,
                )
                added = added + kept * held
            held = added
            y[at, cols] = result
        state[:, cols] = held


def local_scan(x, factors, rates_t, state_in, state_in_t, out_twice, start, skip, chunk):
    rows, channels = x.shape
    groups = factors.shape[0]
    wide = channels // groups
    states = state_in.shape[1]
    whole = lambda shape: pl.BlockSpec(shape, lambda i: (0, 0))
    return pl.pallas_call(
        functools.partial(scan_kernel, chunk),
        out_shape=(
            jax.ShapeDtypeStruct((rows, channels), jnp.float32),
            jax.ShapeDtypeStruct((states, channels), jnp.float32),
        ),
        grid=(groups,),
        in_specs=[
            pl.BlockSpec((rows, wide), lambda i: (0, i)),
            pl.BlockSpec((1,) + factors.shape[1:], lambda i: (i, 0, 0)),
            pl.BlockSpec((GROUP, rows), lambda i: (i, 0)),
            whole(state_in.shape),
            whole(state_in_t.shape),
            whole(out_twice.shape),
            whole(start.shape),
            pl.BlockSpec((1, wide), lambda i: (0, i)),
        ],
        out_specs=(
            pl.BlockSpec((rows, wide), lambda i: (0, i)),
            pl.BlockSpec((states, wide), lambda i: (0, i)),
        ),
        scratch_shapes=[pltpu.VMEM((rows // chunk, chunk, chunk), jnp.float32)],
        cost_estimate=pl.CostEstimate(
            flops=16 * rows * chunk * channels,
            bytes_accessed=8 * x.size,
            transcendentals=rows * chunk * groups * GROUP,
        ),
        name="local_scan",
    )(x, factors, rates_t, state_in, state_in_t, out_twice, start, skip)


def gate_kernel(y, gate, incoming, reach, out_twice, gated, squares):
    rows = y.shape[0]
    lane = lax.broadcasted_iota(jnp.int32, (rows, LANES), 1) < LANES // 2
    folded = jnp.zeros((rows, LANES), jnp.float32)
    for pair in range(GROUP // 2):
        cols = pl.ds(pair * LANES, LANES)
        wide = pair_lanes(
            reach[0, :, pl.ds(2 * pair, 1)], reach[0, :, pl.ds(2 * pair + 1, 1)], lane
        )
        carried = jnp.dot(
            out_twice[...], split_state(incoming[:, cols]), preferred_element_type=jnp.float32
        )
        g = gate[:, cols].astype(jnp.float32)
        value = (y[:, cols] + wide * carried) * (g / (1.0 + jnp.exp(-g)))
        gated[:, cols] = value
        folded = folded + value * value

    @pl.when(pl.program_id(0) == 0)
    def _():
        squares[...] = folded

    @pl.when(pl.program_id(0) > 0)
    def _():
        squares[...] += folded


def gate_all(y, gate, incoming, reach, out_twice):
    rows, channels = y.shape
    groups = reach.shape[0]
    wide = channels // groups
    return pl.pallas_call(
        gate_kernel,
        out_shape=(
            jax.ShapeDtypeStruct((rows, channels), jnp.float32),
            jax.ShapeDtypeStruct((rows, LANES), jnp.float32),
        ),
        grid=(groups,),
        in_specs=[
            pl.BlockSpec((rows, wide), lambda i: (0, i)),
            pl.BlockSpec((rows, wide), lambda i: (0, i)),
            pl.BlockSpec((incoming.shape[0], wide), lambda i: (0, i)),
            pl.BlockSpec((1,) + reach.shape[1:], lambda i: (i, 0, 0)),
            pl.BlockSpec(out_twice.shape, lambda i: (0, 0)),
        ],
        out_specs=(
            pl.BlockSpec((rows, wide), lambda i: (0, i)),
            pl.BlockSpec((rows, LANES), lambda i: (0, 0)),
        ),
        cost_estimate=pl.CostEstimate(
            flops=80 * y.size, bytes_accessed=10 * y.size, transcendentals=y.size
        ),
        name="gate_all",
    )(y, gate, incoming, reach, out_twice)


def layer(
    queries,
    keys,
    values,
    block_plan,
    doc_lengths,
    scan_input,
    gate_input,
    step_size,
    decay_rate,
    state_in,
    state_out,
    skip_gain,
    norm_gain,
):
    ctx, tp = lax.axis_size("ctx"), lax.axis_size("tp")
    me = lax.axis_index("ctx")
    rows = queries.shape[0]
    heads = decay_rate.shape[0]
    channels = scan_input.shape[1]
    head_dim = channels // heads
    groups = heads // GROUP
    kv_heads = keys.shape[1] // HEAD_WIDTH
    chunk = math.gcd(rows, 256)
    chunks = rows // chunk
    doc_reach = longest_reach(ctx)
    key_reach = min(doc_reach, SPAN - 1)

    window = jnp.concatenate([keys, values], axis=1)
    arrived = []
    for by in range(1, key_reach + 1):
        arrived.append(from_behind(window, "ctx", by))

    offsets = jnp.arange(rows, dtype=jnp.int32)
    positions = me * rows + offsets
    doc_ends = jnp.cumsum(doc_lengths)
    start = jnp.sum(
        jnp.where(doc_ends[None, :] <= positions[:, None], doc_lengths[None, :], 0), axis=1
    ).astype(jnp.int32) - me * rows

    step = step_size.astype(jnp.float32)
    rate = (-decay_rate[None, :] * step).reshape(chunks, chunk, heads)
    lower = jnp.tril(jnp.ones((chunk, chunk), jnp.float32))
    cumulative = jnp.einsum("ts,csh->cth", lower, rate, precision=lax.Precision.HIGHEST)
    start_chunks = start.reshape(chunks, chunk)
    first = jnp.arange(chunks, dtype=jnp.int32)[:, None] * chunk
    enters = jnp.where((start_chunks < first)[..., None], jnp.exp(cumulative), 0.0)
    in_tail = offsets.reshape(chunks, chunk) >= start_chunks[:, -1:]
    tails = jnp.where(in_tail[..., None], jnp.exp(cumulative[:, -1:] - cumulative), 0.0)
    through = jnp.ones((heads,), jnp.float32)
    reach = []
    for c in range(chunks):
        reach.append(enters[c] * through[None, :])
        through = through * enters[c, -1]
    reach = jnp.stack(reach).reshape(rows, groups, GROUP).transpose(1, 0, 2)
    flat = cumulative.reshape(rows, heads)
    factors = (
        jnp.stack([flat, enters.reshape(rows, heads), tails.reshape(rows, heads), step], axis=1)
        .reshape(rows, 4, groups, GROUP)
        .transpose(2, 0, 1, 3)
        .reshape(groups, rows, 4 * GROUP)
    )
    out_twice = jnp.concatenate([state_out, state_out], axis=1)
    skip = jnp.repeat(skip_gain, head_dim)[None, :]
    y, end_state = local_scan(
        scan_input,
        factors,
        flat.T,
        state_in,
        state_in.T,
        out_twice,
        start[:, None],
        skip,
        chunk,
    )

    states_n = state_in.shape[1]
    side = jnp.zeros((states_n, -(-heads // LANES) * LANES), jnp.float32).at[0, :heads].set(through)
    packed = jnp.concatenate([end_state, side], axis=1).astype(jnp.bfloat16)
    states = []
    for by in range(1, doc_reach + 1):
        states.append(from_behind(packed, "ctx", by))

    plan_row = lax.dynamic_index_in_dim(block_plan, me, 0, keepdims=False)
    back = jnp.arange(key_reach + 1, dtype=jnp.int32)
    active = (
        jnp.any(plan_row[None, :] == back[:, None], axis=1)
        & (me >= back)
        & (start[0] < -(back - 1) * rows)
    ).astype(jnp.int32)
    blocks = [(keys, values, 0)] + [(kv, kv, kv_heads) for kv in arrived]
    attn_out = attention(queries, blocks, start[None, :], active, kv_heads)

    incoming = states[-1][:, :channels].astype(jnp.float32)
    for state in states[-2::-1]:
        passed = state[0, channels : channels + heads].astype(jnp.float32)
        incoming = (
            state[:, :channels].astype(jnp.float32)
            + jnp.repeat(passed, head_dim)[None, :] * incoming
        )

    gated, squares = gate_all(y, gate_input, incoming, reach, out_twice)
    own = jnp.sum(squares, axis=1).reshape(-1, LANES)
    total = own
    for by in range(1, tp):
        total = total + lax.ppermute(own, "tp", [(i, (i + by) % tp) for i in range(tp)])
    mean = total.reshape(rows) / (channels * tp)
    mamba_out = (gated * lax.rsqrt(mean + 1e-05)[:, None] * norm_gain[None, :]).astype(jnp.bfloat16)
    return (attn_out, mamba_out)


def solution(mesh):
    in_specs = (
        P("ctx", "tp"),
        P("ctx", "tp"),
        P("ctx", "tp"),
        P(),
        P(),
        P("ctx", "tp"),
        P("ctx", "tp"),
        P("ctx", "tp"),
        P("tp"),
        P("ctx", None),
        P("ctx", None),
        P("tp"),
        P("tp"),
    )
    out_specs = (P("ctx", "tp"), P("ctx", "tp"))
    return jax.shard_map(layer, mesh=mesh, in_specs=in_specs, out_specs=out_specs, check_vma=False)
```

```python
import functools
import math

import jax
import jax.numpy as jnp
from jax import lax
from jax.experimental import pallas as pl
from jax.experimental.pallas import tpu as pltpu
from jax.sharding import PartitionSpec as P


HEAD_WIDTH = 128
SPAN = 8
GROUP = 8
LANES = 128
NEG = -1e30


def from_behind(x, axis, by):
    size = lax.axis_size(axis)
    return lax.ppermute(x, axis, [(i, i + by) for i in range(size - by)])


def longest_reach(ctx):
    return min(ctx - 1, 4 if ctx <= SPAN else SPAN)


def pair_lanes(low, high, lane):
    return jnp.where(lane, low, high)


def split_state(state):
    high = state.astype(jnp.bfloat16)
    low = (state - high.astype(jnp.float32)).astype(jnp.bfloat16)
    return jnp.concatenate([high, low], axis=0)


def fold_head(width, keys, value_t, queries, bias, before):
    scale = width**-0.5 * math.log2(math.e)
    scores = lax.dot_general(
        keys, queries, (((1,), (1,)), ((), ())), preferred_element_type=jnp.float32
    )
    scores = scores * scale + bias
    top = jnp.max(scores, axis=0, keepdims=True)
    if before is not None:
        top = jnp.maximum(top, before[0])
    weights = jnp.exp2(scores - top)
    part = jnp.sum(weights, axis=0, keepdims=True)
    weighted = jnp.dot(value_t, weights.astype(jnp.bfloat16), preferred_element_type=jnp.float32)
    if before is not None:
        factor = jnp.exp2(before[0] - top)
        part = part + before[1] * factor
        weighted = weighted + before[2] * factor
    return top, part, weighted


def own_kernel(width, start, q, keys, values, peak, total, acc, bias):
    rows = q.shape[0]
    heads = q.shape[1] // width
    half = rows // 2
    key_at = lax.broadcasted_iota(jnp.int32, (rows, rows), 0)
    query_at = lax.broadcasted_iota(jnp.int32, (rows, rows), 1)
    bias[...] = jnp.where((key_at >= start[...]) & (key_at <= query_at), 0.0, NEG)
    value_t = values[...].T

    def one_head(h, _):
        at = pl.ds(pl.multiple_of(h * width, width), width)
        for lo in (0, half):
            seen = lo + half
            cols = pl.ds(lo, half)
            top, part, weighted = fold_head(
                width, keys[:seen, :], value_t[:, :seen], q[cols, at], bias[:seen, cols], None
            )
            peak[h, :, cols] = top
            total[h, :, cols] = part
            acc[h, :, cols] = weighted
        return 0

    lax.fori_loop(0, heads, one_head, 0, unroll=2)


def attention_kernel(width, pieces, active, start, q, peak_in, total_in, acc_in, *refs):
    keys, values = refs[: 2 * pieces : 2], refs[1 : 2 * pieces : 2]
    out, bias, peak, total, acc = refs[2 * pieces :]
    rows = q.shape[0]
    heads = q.shape[1] // width
    key_at = lax.broadcasted_iota(jnp.int32, (rows, rows), 0)
    peak[...] = peak_in[...]
    total[...] = total_in[...]
    acc[...] = acc_in[...]

    def fold(piece):
        bias[...] = jnp.where(key_at - (piece + 1) * rows >= start[...], 0.0, NEG)
        value_t = values[piece][...].T

        def one_head(h, _):
            at = pl.ds(pl.multiple_of(h * width, width), width)
            peak[h], total[h], acc[h] = fold_head(
                width,
                keys[piece][...],
                value_t,
                q[:, at],
                bias[...],
                (peak[h], total[h], acc[h]),
            )
            return 0

        lax.fori_loop(0, heads, one_head, 0, unroll=2)

    for piece in range(pieces):
        pl.when(active[piece] > 0)(functools.partial(fold, piece))

    def finish(h, _):
        at = pl.ds(pl.multiple_of(h * width, width), width)
        out[:, at] = (acc[h] / total[h]).T.astype(out.dtype)
        return 0

    lax.fori_loop(0, heads, finish, 0)


def attention_sums(rows, heads, kv_heads):
    shapes = [(heads, 1, rows), (heads, 1, rows), (heads, HEAD_WIDTH, rows)]
    specs = [pl.BlockSpec((heads // kv_heads,) + s[1:], lambda i, *a: (i, 0, 0)) for s in shapes]
    return [jax.ShapeDtypeStruct(s, jnp.float32) for s in shapes], specs


def attend_cost(q, blocks):
    return pl.CostEstimate(
        flops=4 * blocks * q.shape[0] * q.size,
        bytes_accessed=8 * q.size,
        transcendentals=blocks * q.shape[0] * q.size // HEAD_WIDTH,
    )


def own_attention(q, keys, values, start, kv_heads):
    rows = q.shape[0]
    wide = q.shape[1] // kv_heads
    shapes, specs = attention_sums(rows, q.shape[1] // HEAD_WIDTH, kv_heads)
    by_head = pl.BlockSpec((rows, HEAD_WIDTH), lambda i: (0, i))
    return pl.pallas_call(
        functools.partial(own_kernel, HEAD_WIDTH),
        out_shape=shapes,
        grid=(kv_heads,),
        in_specs=[
            pl.BlockSpec((1, rows), lambda i: (0, 0)),
            pl.BlockSpec((rows, wide), lambda i: (0, i)),
            by_head,
            by_head,
        ],
        out_specs=specs,
        scratch_shapes=[pltpu.VMEM((rows, rows), jnp.float32)],
        cost_estimate=attend_cost(q, 1),
        name="attend_own",
    )(start, q, keys, values)


def attention(q, sums, blocks, start, active, kv_heads):
    rows = q.shape[0]
    wide = q.shape[1] // kv_heads
    pieces = len(blocks)
    heads = wide // HEAD_WIDTH
    specs = [
        pl.BlockSpec((1, rows), lambda i, a: (0, 0)),
        pl.BlockSpec((rows, wide), lambda i, a: (0, i)),
    ] + attention_sums(rows, q.shape[1] // HEAD_WIDTH, kv_heads)[1]
    operands = [start, q, *sums]
    for block in blocks:
        specs.append(pl.BlockSpec((rows, HEAD_WIDTH), lambda i, a: (0, i)))
        specs.append(pl.BlockSpec((rows, HEAD_WIDTH), lambda i, a: (0, kv_heads + i)))
        operands += [block, block]
    return pl.pallas_call(
        functools.partial(attention_kernel, HEAD_WIDTH, pieces),
        out_shape=jax.ShapeDtypeStruct(q.shape, jnp.bfloat16),
        grid_spec=pltpu.PrefetchScalarGridSpec(
            num_scalar_prefetch=1,
            grid=(kv_heads,),
            in_specs=specs,
            out_specs=pl.BlockSpec((rows, wide), lambda i, a: (0, i)),
            scratch_shapes=[
                pltpu.VMEM((rows, rows), jnp.float32),
                pltpu.VMEM((heads, 1, rows), jnp.float32),
                pltpu.VMEM((heads, 1, rows), jnp.float32),
                pltpu.VMEM((heads, HEAD_WIDTH, rows), jnp.float32),
            ],
        ),
        cost_estimate=attend_cost(q, 3),
        name="attend",
    )(active, *operands)


def scan_kernel(chunk, x, factors, rates_t, state_in, state_in_t, out_twice, start, skip, y, state, mix):
    rows = x.shape[0]
    chunks = rows // chunk
    states = state_in.shape[1]

    @pl.when(pl.program_id(0) == 0)
    def _():
        later = lax.broadcasted_iota(jnp.int32, (chunk, chunk), 0)
        earlier = lax.broadcasted_iota(jnp.int32, (chunk, chunk), 1)
        for c in range(chunks):
            at = pl.ds(c * chunk, chunk)
            both = lax.dot_general(
                out_twice[at, :states],
                state_in[at, :],
                (((1,), (1,)), ((), ())),
                preferred_element_type=jnp.float32,
            )
            seen = (later >= earlier) & (earlier + c * chunk >= start[at, :])
            mix[c] = jnp.where(seen, both, 0.0)

    lane = lax.broadcasted_iota(jnp.int32, (chunk, LANES), 1) < LANES // 2
    lane_row = lax.broadcasted_iota(jnp.int32, (1, LANES), 1) < LANES // 2
    for pair in range(GROUP // 2):
        cols = pl.ds(pair * LANES, LANES)
        a, b = 2 * pair, 2 * pair + 1
        held = None
        for c in range(chunks):
            at = pl.ds(c * chunk, chunk)

            def column(kind, h):
                return factors[0, at, pl.ds(kind * GROUP + h, 1)]

            def wide(kind):
                return pair_lanes(column(kind, a), column(kind, b), lane)

            values = x[at, cols].astype(jnp.float32)
            drive = (wide(3) * values).astype(jnp.bfloat16)

            def local(h):
                gap = jnp.minimum(column(0, h) - rates_t[pl.ds(h, 1), at], 0.0)
                mixing = (jnp.exp(gap) * mix[c]).astype(jnp.bfloat16)
                return jnp.dot(mixing, drive, preferred_element_type=jnp.float32)

            result = pair_lanes(local(a), local(b), lane) + skip[:, cols] * values
            tail = (wide(2) * drive.astype(jnp.float32)).astype(jnp.bfloat16)
            added = jnp.dot(state_in_t[:, at], tail, preferred_element_type=jnp.float32)
            if held is not None:
                result = result + wide(1) * jnp.dot(
                    out_twice[at, :], split_state(held), preferred_element_type=jnp.float32
                )
                last = pl.ds(c * chunk + chunk - 1, 1)
                kept = pair_lanes(
                    factors[0, last, pl.ds(GROUP + a, 1)],
                    factors[0, last, pl.ds(GROUP + b, 1)],
                    lane_row,
                )
                added = added + kept * held
            held = added
            y[at, cols] = result.astype(y.dtype)
        state[:, cols] = held


def local_scan(x, factors, rates_t, state_in, state_in_t, out_twice, start, skip, chunk):
    rows, channels = x.shape
    groups = factors.shape[0]
    wide = channels // groups
    states = state_in.shape[1]
    whole = lambda shape: pl.BlockSpec(shape, lambda i: (0, 0))
    return pl.pallas_call(
        functools.partial(scan_kernel, chunk),
        out_shape=(
            jax.ShapeDtypeStruct((rows, channels), jnp.bfloat16),
            jax.ShapeDtypeStruct((states, channels), jnp.float32),
        ),
        grid=(groups,),
        in_specs=[
            pl.BlockSpec((rows, wide), lambda i: (0, i)),
            pl.BlockSpec((1,) + factors.shape[1:], lambda i: (i, 0, 0)),
            pl.BlockSpec((GROUP, rows), lambda i: (i, 0)),
            whole(state_in.shape),
            whole(state_in_t.shape),
            whole(out_twice.shape),
            whole(start.shape),
            pl.BlockSpec((1, wide), lambda i: (0, i)),
        ],
        out_specs=(
            pl.BlockSpec((rows, wide), lambda i: (0, i)),
            pl.BlockSpec((states, wide), lambda i: (0, i)),
        ),
        scratch_shapes=[pltpu.VMEM((rows // chunk, chunk, chunk), jnp.float32)],
        cost_estimate=pl.CostEstimate(
            flops=16 * rows * chunk * channels,
            bytes_accessed=8 * x.size,
            transcendentals=rows * chunk * groups * GROUP,
        ),
        name="local_scan",
    )(x, factors, rates_t, state_in, state_in_t, out_twice, start, skip)


def gate_kernel(y, gate, incoming, reach, out_twice, gated, squares):
    rows = y.shape[0]
    lane = lax.broadcasted_iota(jnp.int32, (rows, LANES), 1) < LANES // 2
    folded = jnp.zeros((rows, LANES), jnp.float32)
    for pair in range(GROUP // 2):
        cols = pl.ds(pair * LANES, LANES)
        wide = pair_lanes(
            reach[0, :, pl.ds(2 * pair, 1)], reach[0, :, pl.ds(2 * pair + 1, 1)], lane
        )
        carried = jnp.dot(
            out_twice[...], split_state(incoming[:, cols]), preferred_element_type=jnp.float32
        )
        g = gate[:, cols].astype(jnp.float32)
        value = (y[:, cols].astype(jnp.float32) + wide * carried) * (g / (1.0 + jnp.exp(-g)))
        gated[:, cols] = value.astype(gated.dtype)
        folded = folded + value * value

    @pl.when(pl.program_id(0) == 0)
    def _():
        squares[...] = folded

    @pl.when(pl.program_id(0) > 0)
    def _():
        squares[...] += folded


def gate_all(y, gate, incoming, reach, out_twice):
    rows, channels = y.shape
    groups = reach.shape[0]
    wide = channels // groups
    return pl.pallas_call(
        gate_kernel,
        out_shape=(
            jax.ShapeDtypeStruct((rows, channels), jnp.bfloat16),
            jax.ShapeDtypeStruct((rows, LANES), jnp.float32),
        ),
        grid=(groups,),
        in_specs=[
            pl.BlockSpec((rows, wide), lambda i: (0, i)),
            pl.BlockSpec((rows, wide), lambda i: (0, i)),
            pl.BlockSpec((incoming.shape[0], wide), lambda i: (0, i)),
            pl.BlockSpec((1,) + reach.shape[1:], lambda i: (i, 0, 0)),
            pl.BlockSpec(out_twice.shape, lambda i: (0, 0)),
        ],
        out_specs=(
            pl.BlockSpec((rows, wide), lambda i: (0, i)),
            pl.BlockSpec((rows, LANES), lambda i: (0, 0)),
        ),
        cost_estimate=pl.CostEstimate(
            flops=80 * y.size, bytes_accessed=10 * y.size, transcendentals=y.size
        ),
        name="gate_all",
    )(y, gate, incoming, reach, out_twice)


def layer(
    queries,
    keys,
    values,
    block_plan,
    doc_lengths,
    scan_input,
    gate_input,
    step_size,
    decay_rate,
    state_in,
    state_out,
    skip_gain,
    norm_gain,
):
    ctx, tp = lax.axis_size("ctx"), lax.axis_size("tp")
    me = lax.axis_index("ctx")
    rows = queries.shape[0]
    heads = decay_rate.shape[0]
    channels = scan_input.shape[1]
    head_dim = channels // heads
    groups = heads // GROUP
    kv_heads = keys.shape[1] // HEAD_WIDTH
    chunk = math.gcd(rows, 256)
    chunks = rows // chunk
    doc_reach = longest_reach(ctx)
    key_reach = min(doc_reach, SPAN - 1)

    window = jnp.concatenate([keys, values], axis=1)
    arrived = []
    for by in range(1, key_reach + 1):
        arrived.append(from_behind(window, "ctx", by))

    offsets = jnp.arange(rows, dtype=jnp.int32)
    positions = me * rows + offsets
    doc_ends = jnp.cumsum(doc_lengths)
    start = jnp.sum(
        jnp.where(doc_ends[None, :] <= positions[:, None], doc_lengths[None, :], 0), axis=1
    ).astype(jnp.int32) - me * rows

    step = step_size.astype(jnp.float32)
    rate = (-decay_rate[None, :] * step).reshape(chunks, chunk, heads)
    lower = jnp.tril(jnp.ones((chunk, chunk), jnp.float32))
    cumulative = jnp.einsum("ts,csh->cth", lower, rate, precision=lax.Precision.HIGHEST)
    start_chunks = start.reshape(chunks, chunk)
    first = jnp.arange(chunks, dtype=jnp.int32)[:, None] * chunk
    enters = jnp.where((start_chunks < first)[..., None], jnp.exp(cumulative), 0.0)
    in_tail = offsets.reshape(chunks, chunk) >= start_chunks[:, -1:]
    tails = jnp.where(in_tail[..., None], jnp.exp(cumulative[:, -1:] - cumulative), 0.0)
    through = jnp.ones((heads,), jnp.float32)
    reach = []
    for c in range(chunks):
        reach.append(enters[c] * through[None, :])
        through = through * enters[c, -1]
    reach = jnp.stack(reach).reshape(rows, groups, GROUP).transpose(1, 0, 2)
    flat = cumulative.reshape(rows, heads)
    factors = (
        jnp.stack([flat, enters.reshape(rows, heads), tails.reshape(rows, heads), step], axis=1)
        .reshape(rows, 4, groups, GROUP)
        .transpose(2, 0, 1, 3)
        .reshape(groups, rows, 4 * GROUP)
    )
    out_twice = jnp.concatenate([state_out, state_out], axis=1)
    skip = jnp.repeat(skip_gain, head_dim)[None, :]
    y, end_state = local_scan(
        scan_input,
        factors,
        flat.T,
        state_in,
        state_in.T,
        out_twice,
        start[:, None],
        skip,
        chunk,
    )

    states_n = state_in.shape[1]
    side = jnp.zeros((states_n, -(-heads // LANES) * LANES), jnp.float32).at[0, :heads].set(through)
    packed = jnp.concatenate([end_state, side], axis=1).astype(jnp.bfloat16)
    states = []
    for by in range(1, doc_reach + 1):
        states.append(from_behind(packed, "ctx", by))

    plan_row = lax.dynamic_index_in_dim(block_plan, me, 0, keepdims=False)
    back = jnp.arange(1, key_reach + 1, dtype=jnp.int32)
    active = (
        jnp.any(plan_row[None, :] == back[:, None], axis=1)
        & (me >= back)
        & (start[0] < -(back - 1) * rows)
    ).astype(jnp.int32)
    sums = own_attention(queries, keys, values, start[None, :], kv_heads)
    attn_out = attention(queries, sums, arrived, start[None, :], active, kv_heads)

    incoming = states[-1][:, :channels].astype(jnp.float32)
    for state in states[-2::-1]:
        passed = state[0, channels : channels + heads].astype(jnp.float32)
        incoming = (
            state[:, :channels].astype(jnp.float32)
            + jnp.repeat(passed, head_dim)[None, :] * incoming
        )

    gated, squares = gate_all(y, gate_input, incoming, reach, out_twice)
    own = jnp.sum(squares, axis=1).reshape(-1, LANES)
    total = own
    for by in range(1, tp):
        total = total + lax.ppermute(own, "tp", [(i, (i + by) % tp) for i in range(tp)])
    mean = total.reshape(rows) / (channels * tp)
    mamba_out = (gated.astype(jnp.float32) * lax.rsqrt(mean + 1e-05)[:, None] * norm_gain[None, :]).astype(jnp.bfloat16)
    return (attn_out, mamba_out)


def solution(mesh):
    in_specs = (
        P("ctx", "tp"),
        P("ctx", "tp"),
        P("ctx", "tp"),
        P(),
        P(),
        P("ctx", "tp"),
        P("ctx", "tp"),
        P("ctx", "tp"),
        P("tp"),
        P("ctx", None),
        P("ctx", None),
        P("tp"),
        P("tp"),
    )
    out_specs = (P("ctx", "tp"), P("ctx", "tp"))
    return jax.shard_map(layer, mesh=mesh, in_specs=in_specs, out_specs=out_specs, check_vma=False)
```
